32 devices in a mesh: dp: 8 (over z, core), passage: 2 (over x), tensor: 2 (over y).
Axes of the slice: x: 2, y: 2, z: 4, core: 2. Of those that a mesh axis runs over, the one named last changes fastest.
Arguments:
- enc_states: bfloat16 [8, 4, 256, 2048], P('dp', 'passage'), may hold values from -6 to 6
- token_ids: int32 [8, 4, 256], P('dp', 'passage'), may hold values from 0 to 32127, as said below
- assignment: int32 [8, 4], P('dp'), may hold values from 0 to 3, each once within a row
- counts: int32 [8], P('dp'), may hold values from 2 to 4
- dec_states: bfloat16 [8, 32, 2048], P('dp'), may hold values from -210 to 210
- enc_gain: bfloat16 [2048], replicated, may hold values from 0.25 to 1.75
- w_query: bfloat16 [2048, 2048], P(('dp', 'passage'), 'tensor'), may hold values from -0.125 to 0.125
- w_key: bfloat16 [2048, 2048], P(('dp', 'passage'), 'tensor'), may hold values from -0.125 to 0.125
- w_value: bfloat16 [2048, 2048], P(('dp', 'passage'), 'tensor'), may hold values from -0.125 to 0.125
- w_out: bfloat16 [2048, 2048], P('tensor'), may hold values from -0.125 to 0.125
Outputs:
- mixed: bfloat16 [8, 32, 2048], P('dp', None, 'tensor')
The draws below stay inside these ranges and needn't reach their ends.
Inputs may be any that keep to these rules, and one draw needn't show every extreme that they name: `token_ids`: each passage holds nonzero ids followed by zeros, with at least 64 nonzero ids.
All inputs are finite; a program needn't handle non-finite values.
Results may differ from the reference program's by a relative error of at most 0.013.
Values may be sent and summed in bfloat16 or wider, within the bound.
No kernel may reach another device: no remote copies, remote signals or barrier semaphores. Data moves between devices by JAX's collectives and lax.ppermute only.
A program may use at most 64 MiB of HBM per device.

```python
import jax
import jax.numpy as jnp
from jax import lax

D = 2048
HEADS = 32
DH = 64
PLEN = 256
DEC = 32
INNER = 2048
MAXP = 4
QUESTIONS = 8


def draw_token_ids(key, part):
    key_len = jax.random.fold_in(key, 11)
    key_ids = jax.random.fold_in(key, 12)
    lengths = jax.random.randint(key_len, (QUESTIONS, MAXP, 1), PLEN // 4, PLEN + 1)
    ident = jax.random.randint(key_ids, (QUESTIONS, MAXP, PLEN), 1, 32128)
    position = jnp.arange(PLEN, dtype=jnp.int32)[None, None, :]
    return jnp.where(position < lengths, ident, 0).astype(jnp.int32)


def draw_dec_states(key, part):
    key_vals = jax.random.fold_in(key, 22)
    values = jnp.clip(jax.random.normal(key_vals, (QUESTIONS, DEC, D), jnp.float32), -6.0, 6.0)
    return values.astype(jnp.bfloat16)


def set_ends(array, stream_key, low, largest):
    shape = array.shape
    spot = [jax.random.randint(jax.random.fold_in(stream_key, axis), (), 0, shape[axis]) for axis in range(len(shape))]
    array = array.at[tuple(spot)].set(low)
    longest = shape.index(max(shape))
    spot[longest] = (spot[longest] + 1) % shape[longest]
    return array.at[tuple(spot)].set(largest)


def levels(own_key, shape, cuts, least, largest):
    level = 1.0
    for dim, blocks in cuts:
        steps = jax.random.uniform(jax.random.fold_in(jax.random.fold_in(own_key, 6), dim), (blocks,), jnp.float32, least / len(cuts), largest / len(cuts))
        level = level * jnp.repeat(jnp.exp(steps), shape[dim] // blocks).reshape((-1,) + (1,) * (len(shape) - 1 - dim))
    return level


def centred(own_key, shape, scale, bound, split=(), kind=jnp.bfloat16):
    result = jax.random.normal(own_key, shape, jnp.float32) * scale
    if len(split) > 0:
        result = levels(own_key, shape, split, -0.22, 0.18) * result
    return jnp.clip(result, min=-bound, max=bound).astype(kind)


def setup_inputs(seed: int = 0) -> dict:
    key_list = jax.random.split(jax.random.key(seed), 11)
    return {
        "enc_states": centred(key_list[0], (QUESTIONS, MAXP, PLEN, D), 1.0, 6.0, ((0, 8), (1, 2))),
        "token_ids": draw_token_ids(jax.random.fold_in(key_list[10], 71), 0),
        "assignment": jax.vmap(lambda own: jax.random.permutation(own, MAXP))(jax.random.split(key_list[2], QUESTIONS)).reshape((QUESTIONS, MAXP)).astype(jnp.int32),
        "counts": set_ends(jax.random.randint(key_list[3], (QUESTIONS,), MAXP // 2, MAXP + 1), jax.random.fold_in(key_list[3], 1), MAXP // 2, MAXP).astype(jnp.int32),
        "dec_states": draw_dec_states(jax.random.fold_in(key_list[10], 71), 0),
        "enc_gain": jnp.clip(1.0 + 0.15 * jax.random.normal(key_list[5], (D,), jnp.float32), 0.25, 1.75).astype(jnp.bfloat16),
        "w_query": centred(key_list[6], (D, INNER), D ** -0.5, 0.125, ((0, 16), (1, 2))),
        "w_key": centred(key_list[7], (D, INNER), D ** -0.5, 0.125, ((0, 16), (1, 2))),
        "w_value": centred(key_list[8], (D, INNER), D ** -0.5, 0.125, ((0, 16), (1, 2))),
        "w_out": centred(key_list[9], (INNER, D), INNER ** -0.5, 0.125, ((0, 2),)),
    }


def one_question(operands, enc_gain, w_query, w_key, w_value, w_out):
    enc, token_ids, assignment, count, decoder = operands
    flat = enc.reshape(MAXP * PLEN, D).astype(jnp.float32)
    scale_rows = lax.rsqrt(lax.optimization_barrier(jnp.mean(flat * flat, axis=1, keepdims=True)) + 1e-06)
    normed = (flat * scale_rows * enc_gain.astype(jnp.float32)).astype(jnp.bfloat16)
    queries = jnp.dot(decoder, w_query, preferred_element_type=jnp.float32).astype(jnp.bfloat16)
    keys = jnp.dot(normed, w_key, preferred_element_type=jnp.float32).astype(jnp.bfloat16)
    values = jnp.dot(normed, w_value, preferred_element_type=jnp.float32).astype(jnp.bfloat16)
    slot_ids = jnp.arange(MAXP, dtype=jnp.int32)
    used = jnp.arange(MAXP, dtype=jnp.int32) < count
    holds = (assignment[:, None] == slot_ids[None, :]) & used[:, None]
    live_slot = jnp.any(holds, axis=0)
    live = (live_slot[:, None] & (token_ids != 0)).reshape(MAXP * PLEN)
    query_heads = queries.astype(jnp.float32).reshape(DEC, HEADS, DH)
    key_heads = keys.astype(jnp.float32).reshape(MAXP * PLEN, HEADS, DH)
    value_heads = values.astype(jnp.float32).reshape(MAXP * PLEN, HEADS, DH)
    score = jnp.einsum('qhd,khd->hqk', query_heads, key_heads) * DH ** (-0.5)
    score = jnp.where(live[None, None, :], score, jnp.float32(-1e+30))
    top = lax.optimization_barrier(jnp.max(score, axis=2, keepdims=True))
    expo = jnp.where(live[None, None, :], jnp.exp(score - top), jnp.float32(0.0))
    total = lax.optimization_barrier(jnp.sum(expo, axis=2))
    weights = expo.astype(jnp.bfloat16).astype(jnp.float32)
    accum = jnp.einsum('hqk,khd->hqd', weights, value_heads)
    context = (accum / total[:, :, None]).astype(jnp.bfloat16)
    context = jnp.transpose(context, (1, 0, 2)).reshape(DEC, HEADS * DH)
    return jnp.dot(context, w_out, preferred_element_type=jnp.float32).astype(jnp.bfloat16)

def reference(enc_states, token_ids, assignment, counts, dec_states, enc_gain, w_query, w_key, w_value, w_out):

    def step(operands):
        return one_question(operands, enc_gain, w_query, w_key, w_value, w_out)
    return lax.map(step, (enc_states, token_ids, assignment, counts, dec_states))
```

```python
import functools

import jax
import jax.numpy as jnp
from jax import lax
from jax.experimental import pallas as pl
from jax.experimental.pallas import tpu as pltpu
from jax.sharding import PartitionSpec as P

DH = 64
CORES = 2


def ring_order(count):
    even = list(range(0, count, 2))
    odd = list(range(1, count, 2))
    return even + odd[::-1]


def norm_kernel(perm_ref, enc_ref, gain_ref, out_ref):
    flat = enc_ref[...].astype(jnp.float32)
    scale = lax.rsqrt(jnp.mean(flat * flat, axis=1, keepdims=True) + 1e-06)
    width = enc_ref.shape[1]
    block = width // perm_ref.shape[0]
    for j in range(width // block):
        cols = pl.ds(pl.multiple_of(perm_ref[j] * block, 128), block)
        piece = enc_ref[:, cols].astype(jnp.float32) * scale * gain_ref[:, cols].astype(jnp.float32)
        out_ref[:, j * block : (j + 1) * block] = piece.astype(jnp.bfloat16)


def norm_permuted(enc, gain, perm):
    rows, width = enc.shape
    block = width // perm.shape[0]
    if block % 128 == 0:
        tile = min(128, rows)
        return pl.pallas_call(
            norm_kernel,
            grid_spec=pltpu.PrefetchScalarGridSpec(
                num_scalar_prefetch=1,
                grid=(rows // tile,),
                in_specs=[
                    pl.BlockSpec((tile, width), lambda i, p: (i, 0)),
                    pl.BlockSpec((1, width), lambda i, p: (0, 0)),
                ],
                out_specs=pl.BlockSpec((tile, width), lambda i, p: (i, 0)),
            ),
            out_shape=jax.ShapeDtypeStruct((rows, width), jnp.bfloat16),
            name="norm_permuted",
        )(perm, enc, gain[None])
    flat = enc.astype(jnp.float32)
    scale = lax.rsqrt(jnp.mean(flat * flat, axis=1, keepdims=True) + 1e-06)
    normed = (flat * scale * gain.astype(jnp.float32)).astype(jnp.bfloat16)
    return jnp.take(normed.reshape(rows, -1, block), perm, axis=1).reshape(rows, width)


def on_device(
    sizes,
    enc_states,
    token_ids,
    assignment,
    counts,
    dec_states,
    enc_gain,
    w_query,
    w_key,
    w_value,
    w_out,
):
    n_dp, n_pass, n_tens = sizes
    n_z = n_dp // CORES
    slot_count, passage_len, width = enc_states.shape[1:]
    rows = slot_count * passage_len
    depth, columns = w_key.shape
    half = columns // CORES
    heads = half // DH
    dec_len = dec_states.shape[1]
    f32, bf16 = jnp.float32, jnp.bfloat16

    dp = lax.axis_index("dp")
    z, core = dp // CORES, dp % CORES
    px = lax.axis_index("passage")
    ty = lax.axis_index("tensor")

    few = n_pass <= 2
    order = ring_order(n_z)
    source = [[order[(order.index(i) - d) % n_z] for i in range(n_z)] for d in range(n_z)]
    ring = [
        (order[i] * CORES + c, order[(i + 1) % n_z] * CORES + c)
        for i in range(n_z)
        for c in range(CORES)
    ]
    swap = [(i, i ^ 1) for i in range(n_dp)]

    def z_from(d):
        return jnp.asarray(source[d], jnp.int32)[z]

    def to_partner(value):
        return lax.ppermute(value, "dp", swap)

    def z_shift(value, d):
        pairs = [(i, (i + d * CORES) % n_dp) for i in range(n_dp)]
        return lax.ppermute(value, "dp", pairs)

    def x_shift(value, s=1):
        return lax.ppermute(value, "passage", [(i, (i + s) % n_pass) for i in range(n_pass)])

    def own_half(weight):
        return lax.dynamic_slice(weight, (0, core * half), (depth, half))

    def other_half(weight):
        return lax.dynamic_slice(weight, (0, (1 - core) * half), (depth, half))

    def by_core(own, partner):
        first = jnp.where(core == 0, own, partner)
        second = jnp.where(core == 0, partner, own)
        return jnp.concatenate([first, second], axis=0)

    def chip_block(weight):
        return by_core(own_half(weight), to_partner(other_half(weight)))

    decoder = dec_states[0]
    dec_partner = to_partner(decoder)
    q_block = chip_block(w_query)
    k_block = chip_block(w_key)
    v_block = chip_block(w_value)

    def gather(block):
        blocks = []
        here = block
        for d in range(n_z):
            if d > 0:
                here = lax.ppermute(here, "dp", ring)
            if few:
                blocks.append(here)
                for s in range(1, n_pass):
                    blocks.append(x_shift(here, s))
            else:
                blocks.append(lax.all_gather(here, "passage", axis=0, tiled=True))
        return blocks

    k_blocks = gather(k_block)
    v_blocks = gather(v_block)

    perm = jnp.stack(
        [
            (z_from(d) * CORES + c) * n_pass + ((px - s) % n_pass if few else s)
            for d in range(n_z)
            for s in range(n_pass)
            for c in range(CORES)
        ]
    ).astype(jnp.int32)
    normed_own = norm_permuted(enc_states.reshape(rows, width), enc_gain, perm)
    normed = jnp.concatenate([normed_own, to_partner(normed_own)], axis=0)

    slot_ids = px * slot_count + jnp.arange(slot_count, dtype=jnp.int32)
    max_slots = assignment.shape[1]
    used = jnp.arange(max_slots, dtype=jnp.int32) < counts[0]
    holds = (assignment[0][:, None] == slot_ids[None, :]) & used[:, None]
    live_slot = jnp.any(holds, axis=0)
    live_own = (live_slot[:, None] & (token_ids[0] != 0)).reshape(1, rows).astype(f32)
    live = jnp.concatenate([live_own, to_partner(live_own)], axis=0)

    decs = jnp.concatenate([decoder, dec_partner], axis=0)

    def dec_slice(zz):
        starts = [((zz * CORES + c) * n_pass + px) * depth for c in range(CORES)]
        return jnp.concatenate(
            [lax.dynamic_slice(decs, (0, s), (CORES * dec_len, depth)) for s in starts], axis=1
        )

    arrived = [dec_slice(z)] + [z_shift(dec_slice((z + d) % n_z), d) for d in range(1, n_z)]
    q_part = jnp.dot(jnp.concatenate(arrived, axis=0), q_block, preferred_element_type=f32)
    q_part = q_part.reshape(n_z, CORES * dec_len, half)
    q_sum = q_part[0]
    for d in range(1, n_z):
        q_sum = q_sum + z_shift(q_part[d], n_z - d)
    q_all = q_sum
    if few:
        for s in range(1, n_pass):
            q_all = q_all + x_shift(q_sum, s)
    else:
        q_all = lax.psum(q_sum, "passage")
    queries = q_all.astype(bf16).reshape(CORES, dec_len, heads, DH)

    def project(blocks):
        total = None
        size = blocks[0].shape[0]
        for i, block in enumerate(blocks):
            part = jnp.dot(
                normed[:, i * size : (i + 1) * size], block, preferred_element_type=f32
            )
            total = part if total is None else total + part
        return total.astype(bf16).reshape(CORES, rows, heads, DH)

    keys = project(k_blocks)
    alive = (live != 0)[:, None, None, :]
    score = jnp.einsum("bqhd,bkhd->bhqk", queries, keys, preferred_element_type=f32) * DH ** (-0.5)
    score = jnp.where(alive, score, f32(-1e30))
    top = jnp.max(score, axis=3)
    expo = jnp.where(alive, jnp.exp(score - top[..., None]), f32(0.0))
    total = jnp.sum(expo, axis=3)

    stats = jnp.stack([top, total])
    if few:
        parts = [stats] + [x_shift(stats, s) for s in range(1, n_pass)]
    else:
        gathered = lax.all_gather(stats, "passage")
        parts = [gathered[s] for s in range(n_pass)]
    top_all = functools.reduce(jnp.maximum, [p[0] for p in parts])
    total_all = sum(p[1] * jnp.exp(p[0] - top_all) for p in parts)
    factor = jnp.exp(top - top_all) / total_all

    out_cols = w_out.shape[1] // n_tens

    def out_piece(c, t):
        return lax.dynamic_slice(w_out, (c * half, t * out_cols), (half, out_cols))

    out_rows = [out_piece(core, ty), out_piece(1 - core, ty)]
    for s in range(1, n_tens):
        pairs = [(i, (i + s) % n_tens) for i in range(n_tens)]
        mine = lax.ppermute(out_piece(core, (ty + s) % n_tens), "tensor", pairs)
        out_rows += [mine, to_partner(mine)]
    w_mixed = jnp.concatenate(out_rows, axis=0)

    values = project(v_blocks)
    accum = jnp.einsum(
        "bhqk,bkhd->bhqd", expo.astype(bf16), values, preferred_element_type=f32
    )
    share = accum * factor[..., None]
    if not few:
        share = lax.psum(share, "passage")
    share = share.astype(bf16)
    share = jnp.transpose(share, (0, 2, 1, 3)).reshape(CORES, dec_len, half)

    def moved(value, flip, s, t):
        if (flip, s, t) == (0, 0, 0):
            return value
        pairs = []
        for i in range(n_dp):
            for j in range(n_pass):
                for k in range(n_tens):
                    here = (i * n_pass + j) * n_tens + k
                    there = ((i ^ flip) * n_pass + (j + s) % n_pass) * n_tens + (k + t) % n_tens
                    pairs.append((here, there))
        return lax.ppermute(value, ("dp", "passage", "tensor"), pairs)

    context = []
    for t in range(n_tens):
        for flip in range(CORES):
            shifts = range(n_pass if few else 1)
            pieces = [moved(share[flip], flip, s, t).astype(f32) for s in shifts]
            context.append(sum(pieces).astype(bf16))
    mixed = jnp.dot(jnp.concatenate(context, axis=1), w_mixed, preferred_element_type=f32)
    return mixed.astype(bf16)[None]


def solution(mesh):
    sizes = (mesh.shape["dp"], mesh.shape["passage"], mesh.shape["tensor"])
    return jax.shard_map(
        functools.partial(on_device, sizes),
        mesh=mesh,
        in_specs=(
            P("dp", "passage", None, None),
            P("dp", "passage", None),
            P("dp", None),
            P("dp"),
            P("dp", None, None),
            P(),
            P(("dp", "passage"), "tensor"),
            P(("dp", "passage"), "tensor"),
            P(("dp", "passage"), "tensor"),
            P("tensor", None),
        ),
        out_specs=P("dp", None, "tensor"),
        check_vma=False,
    )
```
